32 devices in a mesh: dp: 4 (over y, core), blk: 4 (over z), ulysses: 2 (over x).
Axes of the slice: x: 2, y: 2, z: 4, core: 2. Of those that a mesh axis runs over, the one named last changes fastest.
Arguments:
- queries: bfloat16 [24576, 2048], P(('dp', 'blk', 'ulysses')), parts along dimension 0, may hold values from -128 to 128
- keys: bfloat16 [24576, 2048], P(('dp', 'blk', 'ulysses')), parts along dimension 0, may hold values from -6 to 6
- values: bfloat16 [24576, 2048], P(('dp', 'blk', 'ulysses')), parts along dimension 0, may hold values from -6 to 6
- rel_bias: float32 [16, 27], replicated, may hold values from -4 to 4
- tile_lists: int32 [16, 8], replicated, may hold values from 0 to 16, as said below
- tile_pos: int32 [16], replicated, may hold values from 0 to 3, as said below
Outputs:
- attended: bfloat16 [24576, 2048], P(('dp', 'blk', 'ulysses')), parts along dimension 0
The draws below stay inside these ranges and needn't reach their ends.
There are 4 independent parts, one for each index of `dp`. The reference program is written for one: setup_inputs(seed, part) draws one part's arguments, and reference() takes and returns one part's arrays. A program takes and returns all parts, laid end to end along the dimension named above; an argument that names none is the same for every part. Nothing has to cross between parts.
Inputs may be any that keep to these rules, and one draw needn't show every extreme that they name: `tile_lists`: row t names the key tiles of query tile t, each once: t itself first, then tiles of t's frame or of the frames just before and after it (frame = tile // 4); named tiles come first and 16 fills the rest of the row. `tile_pos`: the cell (row * 2 + column) of each tile within its frame; the tiles of one frame take each cell once.
All inputs are finite; a program needn't handle non-finite values.
Results may differ from the reference program's by a relative error of at most 0.0035.
Values may be sent and summed in bfloat16 or wider, within the bound.
A program may use at most 128 MiB of HBM per device.

```python
import math
import jax
import jax.numpy as jnp
from jax import lax

H = 16
DH = 128
TILE = 384
GH = 2
GW = 2
NBR = 8
QW = 2048
NFRAMES = 4
NT = 16
SEQ = 6144


def query_key_pair(key):
    base_keys = jnp.clip(jax.random.normal(jax.random.fold_in(key, 101), (SEQ, QW), jnp.float32), -6.0, 6.0)
    base_queries = jnp.clip(3.0 * jax.random.normal(jax.random.fold_in(key, 202), (SEQ, QW), jnp.float32), -18.0, 18.0)
    return (base_queries, base_keys)


def draw_queries(key, part):
    return query_key_pair(key)[0].astype(jnp.bfloat16)


def draw_keys(key, part):
    return query_key_pair(key)[1].astype(jnp.bfloat16)


def draw_tile_lists(key, part):
    frame_tiles = GH * GW
    tile_ids = jnp.arange(NT, dtype=jnp.int32)
    frame_of = tile_ids // frame_tiles
    candidate = jnp.arange(3 * frame_tiles, dtype=jnp.int32)
    cand_frame = frame_of[:, None] - 1 + candidate[None, :] // frame_tiles
    cand_tile = cand_frame * frame_tiles + candidate[None, :] % frame_tiles
    inside = (cand_frame >= 0) & (cand_frame < NFRAMES)
    random_part = jax.random.randint(jax.random.fold_in(key, 1), (NT, 3 * frame_tiles), 0, 65536)
    ranking = random_part * (3 * frame_tiles) + candidate[None, :]
    ranking = jnp.where(cand_tile == tile_ids[:, None], 2 ** 30, ranking)
    ranking = jnp.where(inside, ranking, -1)
    order = jnp.argsort(-ranking, axis=1)
    sorted_tiles = jnp.take_along_axis(cand_tile, order, axis=1)
    heavy = jax.random.randint(jax.random.fold_in(key, 2), (NFRAMES,), 0, 4) == 0
    heavy = heavy | (jnp.arange(NFRAMES) == 1)
    light = jax.random.randint(jax.random.fold_in(key, 3), (NT,), 3, 6)
    wanted = jnp.where(heavy[frame_of], NBR, light)
    available = jnp.sum(inside.astype(jnp.int32), axis=1)
    wanted = jnp.minimum(wanted, available)
    slot_ids = jnp.arange(NBR)
    return jnp.where(slot_ids[None, :] < wanted[:, None], sorted_tiles[:, :NBR], NT).astype(jnp.int32)


def draw_tile_pos(key, part):
    frame_tiles = GH * GW
    ranking = jax.random.randint(jax.random.fold_in(key, 7), (NFRAMES, frame_tiles), 0, 65536) * frame_tiles
    ranking = ranking + jnp.arange(frame_tiles)[None, :]
    return jnp.argsort(ranking, axis=1).astype(jnp.int32).reshape(NT)


def shard_levels(stream_key, extent, cuts, smallest, top_value):
    level = 1.0
    for dim, blocks in cuts:
        heights = jax.random.uniform(jax.random.fold_in(jax.random.fold_in(stream_key, 6), dim), (blocks,), jnp.float32, smallest / len(cuts), top_value / len(cuts))
        level = level * jnp.repeat(jnp.exp(heights), extent[dim] // blocks).reshape((-1,) + (1,) * (len(extent) - 1 - dim))
    return level


def normal_values(rng, dims, spread, bound, cuts=(), kind=jnp.bfloat16):
    entries = jax.random.normal(rng, dims, jnp.float32) * spread
    if len(cuts) > 0:
        entries = shard_levels(rng, dims, cuts, -0.22, 0.18) * entries
    return jnp.clip(entries, min=-bound, max=bound).astype(kind)


def setup_inputs(seed: int = 0, part: int = 0) -> dict:
    splits = jax.random.split(jax.random.key(seed), 7)
    own_keys = jax.random.split(jax.random.fold_in(splits[6], part), 7)
    queries = draw_queries(jax.random.fold_in(jax.random.fold_in(splits[6], part), 71), part)
    keys = draw_keys(jax.random.fold_in(jax.random.fold_in(splits[6], part), 71), part)
    values = normal_values(own_keys[2], (SEQ, QW), 1.0, 6.0, ((0, 8),))
    rel_bias = normal_values(splits[3], (H, 27), 1.0, 4.0, (), jnp.float32)
    tile_lists = draw_tile_lists(jax.random.fold_in(splits[6], 71), part)
    tile_pos = draw_tile_pos(jax.random.fold_in(splits[6], 71), part)
    return dict(queries=queries, keys=keys, values=values, rel_bias=rel_bias, tile_lists=tile_lists, tile_pos=tile_pos)


def reference(queries, keys, values, rel_bias, tile_lists, tile_pos):
    frame_tiles = GH * GW
    query_tiles = queries.reshape(NT, TILE, H, DH)
    key_tiles = keys.reshape(NT, TILE, H, DH)
    value_tiles = values.reshape(NT, TILE, H, DH)
    frame_of = jnp.arange(NT, dtype=jnp.int32) // frame_tiles
    inv_root = 1.0 / math.sqrt(DH)

    def one_tile(tile_index):
        listed = tile_lists[tile_index]
        valid = listed < NT
        safe_ids = jnp.where(valid, listed, 0).astype(jnp.int32)
        key_block = key_tiles[safe_ids].astype(jnp.float32)
        value_block = value_tiles[safe_ids].astype(jnp.float32)
        query_tile = query_tiles[tile_index].astype(jnp.float32)
        scores = jnp.einsum('ihd,njhd->ihnj', query_tile, key_block) * inv_root
        query_cell = tile_pos[tile_index]
        key_cell = tile_pos[safe_ids]
        offset = (frame_of[safe_ids] - frame_of[tile_index] + 1) * 9
        offset = offset + (key_cell // GW - query_cell // GW + 1) * 3
        offset = offset + (key_cell % GW - query_cell % GW + 1)
        offset = jnp.clip(offset, 0, 26).astype(jnp.int32)
        head_bias = rel_bias[:, offset]
        scores = scores + head_bias[None, :, :, None]
        keep_mask = valid[None, None, :, None]
        scores = jnp.where(keep_mask, scores, -1e+30)
        row_max = lax.optimization_barrier(jnp.max(scores, axis=(2, 3), keepdims=True))
        weights = jnp.where(keep_mask, jnp.exp(scores - row_max), 0.0)
        row_total = lax.optimization_barrier(jnp.sum(weights, axis=(2, 3)))
        rounded = lax.optimization_barrier(weights.astype(jnp.bfloat16)).astype(jnp.float32)
        mixed = jnp.einsum('ihnj,njhd->ihd', rounded, value_block) / row_total[..., None]
        return mixed.astype(jnp.bfloat16)
    attended = lax.map(one_tile, jnp.arange(NT, dtype=jnp.int32))
    return attended.reshape(SEQ, QW)
```

```python
import functools
import math

import jax
import jax.numpy as jnp
from jax import lax
from jax.experimental import pallas as pl
from jax.experimental.pallas import tpu as pltpu
from jax.sharding import PartitionSpec as P

H = 16
DH = 128
TILE = 384
GH = 2
GW = 2
LOG2E = 1.4426950408889634


def attention_kernel(n, heads, tokens, frame_tokens, *refs):
    rank_ref, lists_ref, counts_ref, bias_ref = refs[:4]
    ins = refs[4 : 4 + 4 * n]
    outs = refs[4 + 4 * n : 4 + 5 * n]
    q_buf, k_buf, v_buf, o_buf, s_buf, acc, sems = refs[4 + 5 * n :]
    rank = rank_ref[0]
    scale = LOG2E / math.sqrt(DH)

    copies = []
    for d in range(n):
        source = lax.rem(rank + (n - d), n)
        start = pl.multiple_of(source * tokens, tokens)
        copies.append((ins[d], q_buf.at[pl.ds(start, tokens)]))
        for f in range(3):
            kv = ins[n * (1 + f) + d]
            at = pl.ds(pl.multiple_of(f * frame_tokens + start, tokens), tokens)
            copies.append((kv.at[0], k_buf.at[at]))
            copies.append((kv.at[1], v_buf.at[at]))
    copies = [pltpu.make_async_copy(a, b, sems.at[i]) for i, (a, b) in enumerate(copies)]
    for copy in copies:
        copy.start()
    for copy in copies:
        copy.wait()

    ones = jnp.ones((TILE, DH), jnp.bfloat16)

    def tile_body(t, _):
        rows = pl.ds(pl.multiple_of(t * TILE, TILE), TILE)
        count = counts_ref[t]

        def score_slot(i, tops):
            keys = pl.ds(pl.multiple_of(lists_ref[t, i] * TILE, TILE), TILE)
            new_tops = []
            for h in range(heads):
                lanes = slice(h * DH, (h + 1) * DH)
                s = lax.dot_general(
                    q_buf[rows, lanes],
                    k_buf[keys, lanes],
                    (((1,), (1,)), ((), ())),
                    preferred_element_type=jnp.float32,
                )
                s = s * scale + bias_ref[t, i, h]
                s_buf[h, i] = s
                top = jnp.maximum(s[:, :DH], s[:, DH : 2 * DH])
                for c in range(2, TILE // DH):
                    top = jnp.maximum(top, s[:, c * DH : (c + 1) * DH])
                new_tops.append(jnp.maximum(tops[h], top))
            return tuple(new_tops)

        tops = lax.fori_loop(
            0, count, score_slot, tuple(jnp.full((TILE, DH), -jnp.inf, jnp.float32) for _ in range(heads))
        )
        tops = tuple(
            jnp.broadcast_to(jnp.max(top, axis=1, keepdims=True), (TILE, DH)) for top in tops
        )
        for h in range(heads):
            acc[h] = jnp.zeros((TILE, 2 * DH), jnp.float32)

        def mix_slot(i, tops):
            keys = pl.ds(pl.multiple_of(lists_ref[t, i] * TILE, TILE), TILE)
            for h in range(heads):
                lanes = slice(h * DH, (h + 1) * DH)
                top = jnp.concatenate([tops[h]] * (TILE // DH), axis=1)
                weights = jnp.exp2(s_buf[h, i] - top).astype(jnp.bfloat16)
                value = jnp.concatenate([v_buf[keys, lanes], ones], axis=1)
                acc[h] += jnp.dot(weights, value, preferred_element_type=jnp.float32)
            return tops

        lax.fori_loop(0, count, mix_slot, tops)
        for h in range(heads):
            o_buf[rows, h * DH : (h + 1) * DH] = (acc[h, :, :DH] / acc[h, :, DH:]).astype(jnp.bfloat16)
        return 0

    lax.fori_loop(0, frame_tokens // TILE, tile_body, 0)

    copies = []
    for d in range(n):
        target = lax.rem(rank + d, n)
        at = pl.ds(pl.multiple_of(target * tokens, tokens), tokens)
        copies.append(pltpu.make_async_copy(o_buf.at[at], outs[d], sems.at[d]))
    for copy in copies:
        copy.start()
    for copy in copies:
        copy.wait()


def attend(n, heads, tokens, frame_tokens, slots, pairs, scalars, pieces):
    cols = heads * DH
    smem = pl.BlockSpec(memory_space=pltpu.SMEM)
    hbm = pl.BlockSpec(memory_space=pl.ANY)
    return pl.pallas_call(
        functools.partial(attention_kernel, n, heads, tokens, frame_tokens),
        out_shape=[jax.ShapeDtypeStruct((tokens, cols), jnp.bfloat16)] * n,
        in_specs=[smem] * 4 + [hbm] * (4 * n),
        out_specs=[hbm] * n,
        scratch_shapes=[
            pltpu.VMEM((frame_tokens, cols), jnp.bfloat16),
            pltpu.VMEM((3 * frame_tokens, cols), jnp.bfloat16),
            pltpu.VMEM((3 * frame_tokens, cols), jnp.bfloat16),
            pltpu.VMEM((frame_tokens, cols), jnp.bfloat16),
            pltpu.VMEM((heads, slots, TILE, TILE), jnp.float32),
            pltpu.VMEM((heads, TILE, 2 * DH), jnp.float32),
            pltpu.SemaphoreType.DMA((7 * n,)),
        ],
        compiler_params=pltpu.CompilerParams(vmem_limit_bytes=40 * 1024 * 1024),
        cost_estimate=pl.CostEstimate(
            flops=pairs * heads * TILE * TILE * DH * 16, bytes_accessed=7 * frame_tokens * cols * 2,
            transcendentals=pairs * heads * TILE * TILE,
        ),
        name="attend",
    )(*scalars, *pieces)


def on_device(queries, keys, values, rel_bias, tile_lists, tile_pos):
    n = lax.axis_size("ulysses")
    blk_count = lax.axis_size("blk")
    blk_rank = lax.axis_index("blk")
    rank = lax.axis_index("ulysses")
    heads_dev = H // n
    head_cols = heads_dev * DH
    groups = min(4, heads_dev)
    heads = heads_dev // groups
    cols = heads * DH
    tokens = queries.shape[0]
    frame_tokens = tokens * n
    frame_tiles = frame_tokens // TILE
    total_tiles, slots = tile_lists.shape

    my_lists = lax.dynamic_slice_in_dim(tile_lists, blk_rank * frame_tiles, frame_tiles, 0)
    valid = my_lists < total_tiles
    counts = jnp.sum(valid.astype(jnp.int32), axis=1)
    safe = jnp.where(valid, my_lists, 0)
    local = jnp.where(valid, my_lists - (blk_rank - 1) * frame_tiles, 0)
    key_cell = tile_pos[safe]
    query_cell = lax.dynamic_slice_in_dim(tile_pos, blk_rank * frame_tiles, frame_tiles, 0)[:, None]
    offset = (safe // frame_tiles - blk_rank + 1) * 9
    offset = offset + (key_cell // GW - query_cell // GW + 1) * 3
    offset = offset + (key_cell % GW - query_cell % GW + 1)
    offset = jnp.clip(offset, 0, 26)
    table = lax.dynamic_slice_in_dim(rel_bias, rank * heads_dev, heads_dev, 0) * LOG2E
    bias = jnp.transpose(table[:, offset], (1, 2, 0))
    rank_arr = jnp.reshape(rank, (1,)).astype(jnp.int32)

    def cut(x, d, g):
        col = lax.rem(rank + d, n) * head_cols + g * cols
        return lax.dynamic_slice(x, (0, col), (tokens, cols))

    def across(x, d):
        return lax.ppermute(x, "ulysses", [(i, (i + d) % n) for i in range(n)])

    def up(x):
        return lax.ppermute(x, "blk", [(i, i + 1) for i in range(blk_count - 1)])

    def down(x):
        return lax.ppermute(x, "blk", [(i + 1, i) for i in range(blk_count - 1)])

    def after_of(x, *others):
        return lax.optimization_barrier((x, *others))[0]

    kv_own, kv_all, q_all = [], [], []
    source = (keys, values)
    for g in range(groups):
        sent = []
        for d in range(1, n):
            pack = jnp.stack((cut(source[0], d, g), cut(source[1], d, g)))
            source = lax.optimization_barrier((*source, pack))[:2]
            sent.append(across(pack, d))
        own = jnp.stack((cut(source[0], 0, g), cut(source[1], 0, g)))
        if g > 0:
            own = after_of(own, *kv_all[g - 1][1:])
        else:
            source = lax.optimization_barrier((*source, own))[:2]
        kv_all.append([own] + sent)
    source = queries
    for g in range(groups):
        pieces = []
        for d in range(n):
            piece = cut(source, d, g)
            source = after_of(source, piece)
            pieces.append(across(piece, d) if d else piece)
        q_all.append(pieces)

    placed = []
    for g in range(groups):
        kv, q = kv_all[g], q_all[g]
        before = [up(piece) for piece in kv]
        after = [down(piece) for piece in kv]
        out = attend(
            n, heads, tokens, frame_tokens, slots, frame_tiles * slots,
            (rank_arr, local, counts, bias[:, :, g * heads : (g + 1) * heads]),
            (*q, *before, *kv, *after),
        )
        placed.append([out[0]] + [across(out[d], d) for d in range(1, n)])
    result = jnp.zeros((tokens, n * head_cols), jnp.bfloat16)
    for g in range(groups):
        for d in range(n):
            col = lax.rem(rank + (n - d), n) * head_cols + g * cols
            result = lax.dynamic_update_slice(result, placed[g][d], (0, col))
    return result


def solution(mesh):
    return jax.shard_map(
        on_device,
        mesh=mesh,
        in_specs=(
            P(("dp", "blk", "ulysses"), None),
            P(("dp", "blk", "ulysses"), None),
            P(("dp", "blk", "ulysses"), None),
            P(),
            P(),
            P(),
        ),
        out_specs=P(("dp", "blk", "ulysses"), None),
        check_vma=False,
    )
```

```python
import functools
import math

import jax
import jax.numpy as jnp
from jax import lax
from jax.experimental import pallas as pl
from jax.experimental.pallas import tpu as pltpu
from jax.sharding import PartitionSpec as P

H = 16
DH = 128
TILE = 384
GH = 2
GW = 2
LOG2E = 1.4426950408889634
MESH = pl.DeviceIdType.MESH


def attention_kernel(n, blk_count, groups, tokens, slots, *refs):
    lists_ref, bias_ref, q_ref, k_ref, v_ref, out_ref = refs[:6]
    k_bufs = refs[6 : 6 + groups]
    v_bufs = refs[6 + groups : 6 + 2 * groups]
    q_bufs = refs[6 + 2 * groups : 6 + 3 * groups]
    o_bufs = refs[6 + 3 * groups : 6 + 4 * groups]
    s_buf, acc, local_sems, x_send, x_recv, z_send, z_recv, o_send, o_recv = refs[6 + 4 * groups :]
    frame = tokens * n
    head_cols = groups * DH
    rank = lax.axis_index("ulysses")
    blk = lax.axis_index("blk")
    has_up = blk < blk_count - 1
    has_down = blk > 0
    scale = LOG2E / math.sqrt(DH)
    inputs = (k_ref, v_ref, q_ref)

    unit = math.gcd(tokens, TILE)
    parts = TILE // unit

    def rows(frame_index, owner):
        return pl.ds(frame_index * (frame // unit) + owner * (tokens // unit), tokens // unit)

    def flat(owner):
        return pl.ds(pl.multiple_of(owner * tokens, 64), tokens)

    def lanes(owner, g):
        return pl.ds(pl.multiple_of(owner * head_cols + g * DH, DH), DH)

    def cut(which, owner, g):
        if which == 2:
            return q_ref.at[:, lanes(owner, g)]
        return inputs[which].at[:, :, lanes(owner, g)]

    def home(which, g, owner):
        if which == 2:
            return q_bufs[g].at[flat(owner)]
        return (k_bufs, v_bufs)[which][g].at[rows(1, owner)]

    def local(which, g):
        return pltpu.make_async_copy(
            cut(which, rank, g), home(which, g, rank), local_sems.at[which, g]
        )

    def across(which, g, d):
        target = lax.rem(rank + d, n)
        return pltpu.make_async_remote_copy(
            src_ref=cut(which, target, g),
            dst_ref=home(which, g, rank),
            send_sem=x_send.at[which, g, d],
            recv_sem=x_recv.at[which, g, d],
            device_id={"ulysses": target},
            device_id_type=MESH,
        )

    def halo(which, g, d, way):
        owner = lax.rem(rank + (n - d), n)
        source = home(which, g, owner) if d else cut(which, rank, g)
        return pltpu.make_async_remote_copy(
            src_ref=source,
            dst_ref=(k_bufs, v_bufs)[which][g].at[rows(2 * way, owner)],
            send_sem=z_send.at[way, which, g, d],
            recv_sem=z_recv.at[way, which, g, d],
            device_id={"blk": blk - 1 if way else blk + 1},
            device_id_type=MESH,
        )

    def give(g, d):
        target = lax.rem(rank + d, n)
        return pltpu.make_async_remote_copy(
            src_ref=o_bufs[g].at[flat(target)],
            dst_ref=out_ref.at[:, lanes(rank, g)],
            send_sem=o_send.at[g, d],
            recv_sem=o_recv.at[g, d],
            device_id={"ulysses": target},
            device_id_type=MESH,
        )

    def keep(g):
        return pltpu.make_async_copy(
            o_bufs[g].at[flat(rank)], out_ref.at[:, lanes(rank, g)], o_send.at[g, 0]
        )

    def start_halo(g, ds):
        for way, present in ((0, has_up), (1, has_down)):
            @pl.when(present)
            def _():
                for d in ds:
                    for which in range(2):
                        halo(which, g, d, way).start()

    def relay(g):
        for d in range(1, n):
            for which in range(2):
                across(which, g, d).wait_recv()
        start_halo(g, range(1, n))

    barrier = pltpu.get_barrier_semaphore()
    for d in range(1, n):
        pl.semaphore_signal(
            barrier, inc=1, device_id={"ulysses": lax.rem(rank + d, n)}, device_id_type=MESH
        )
    @pl.when(has_up)
    def _():
        pl.semaphore_signal(barrier, inc=1, device_id={"blk": blk + 1}, device_id_type=MESH)
    @pl.when(has_down)
    def _():
        pl.semaphore_signal(barrier, inc=1, device_id={"blk": blk - 1}, device_id_type=MESH)
    below = (blk + blk_count - 1) // blk_count
    above = (2 * blk_count - 2 - blk) // blk_count
    pl.semaphore_wait(barrier, n - 1 + below + above)

    for g in range(groups):
        for which in range(3):
            for d in range(1, n):
                across(which, g, d).start()
        if g == 0:
            start_halo(0, range(1))
    for g in range(groups):
        for which in range(3):
            local(which, g).start()
    relay(0)
    if groups > 1:
        start_halo(1, range(1))

    pairs = slots // 2
    ones = jnp.ones((2 * TILE, DH), jnp.bfloat16)

    def compute(g):
        k_buf, v_buf, q_buf, o_buf = k_bufs[g], v_bufs[g], q_bufs[g], o_bufs[g]

        def listed(buf, t, p):
            return jnp.concatenate(
                [
                    buf[lists_ref[t, 2 * p + i] * parts + j]
                    for i in range(2)
                    for j in range(parts)
                ],
                axis=0,
            )

        def tile_body(t, _):
            here = pl.ds(pl.multiple_of(t * TILE, TILE), TILE)

            def score_pair(p, top):
                s = lax.dot_general(
                    q_buf[here, :],
                    listed(k_buf, t, p),
                    (((1,), (1,)), ((), ())),
                    preferred_element_type=jnp.float32,
                )
                s = jnp.concatenate(
                    [
                        s[:, i * TILE : (i + 1) * TILE] * scale + bias_ref[t, 2 * p + i, g]
                        for i in range(2)
                    ],
                    axis=1,
                )
                s_buf[p] = s
                for c in range(2 * TILE // DH):
                    top = jnp.maximum(top, s[:, c * DH : (c + 1) * DH])
                return top

            top = lax.fori_loop(0, pairs, score_pair, jnp.full((TILE, DH), -3e38, jnp.float32))
            top = jnp.broadcast_to(jnp.max(top, axis=1, keepdims=True), (TILE, DH))
            acc[...] = jnp.zeros((TILE, 2 * DH), jnp.float32)

            def mix_pair(p, top):
                wide = jnp.concatenate([top] * (2 * TILE // DH), axis=1)
                weights = jnp.exp2(s_buf[p] - wide).astype(jnp.bfloat16)
                value = jnp.concatenate([listed(v_buf, t, p), ones], axis=1)
                acc[...] += jnp.dot(weights, value, preferred_element_type=jnp.float32)
                return top

            lax.fori_loop(0, pairs, mix_pair, top)
            o_buf[here, :] = (acc[:, :DH] / acc[:, DH:]).astype(jnp.bfloat16)
            return 0

        lax.fori_loop(0, frame // TILE, tile_body, 0)

    for g in range(groups):
        if g + 1 < groups:
            relay(g + 1)
        if g + 2 < groups:
            start_halo(g + 2, range(1))
        for which in range(3):
            local(which, g).wait()
        for d in range(1, n):
            across(2, g, d).wait_recv()
        for way, present in ((0, has_down), (1, has_up)):
            @pl.when(present)
            def _():
                for d in range(n):
                    for which in range(2):
                        halo(which, g, d, way).wait_recv()
        compute(g)
        for d in range(1, n):
            give(g, d).start()
        keep(g).start()

    for g in range(groups):
        for d in range(1, n):
            for which in range(3):
                across(which, g, d).wait_send()
            give(g, d).wait()
        keep(g).wait()
        for way, present in ((0, has_up), (1, has_down)):
            @pl.when(present)
            def _():
                for d in range(n):
                    for which in range(2):
                        halo(which, g, d, way).wait_send()


def on_device(queries, keys, values, rel_bias, tile_lists, tile_pos):
    n = lax.axis_size("ulysses")
    blk_count = lax.axis_size("blk")
    blk_rank = lax.axis_index("blk")
    rank = lax.axis_index("ulysses")
    groups = H // n
    tokens = queries.shape[0]
    frame_tokens = tokens * n
    frame_tiles = frame_tokens // TILE
    total_tiles, slots = tile_lists.shape

    my_lists = lax.dynamic_slice_in_dim(tile_lists, blk_rank * frame_tiles, frame_tiles, 0)
    valid = my_lists < total_tiles
    own = blk_rank * frame_tiles + jnp.arange(frame_tiles, dtype=jnp.int32)[:, None]
    safe = jnp.where(valid, my_lists, own)
    local = safe - (blk_rank - 1) * frame_tiles
    key_cell = tile_pos[safe]
    query_cell = lax.dynamic_slice_in_dim(tile_pos, blk_rank * frame_tiles, frame_tiles, 0)[:, None]
    offset = (safe // frame_tiles - blk_rank + 1) * 9
    offset = offset + (key_cell // GW - query_cell // GW + 1) * 3
    offset = offset + (key_cell % GW - query_cell % GW + 1)
    offset = jnp.clip(offset, 0, 26)
    table = lax.dynamic_slice_in_dim(rel_bias, rank * groups, groups, 0) * LOG2E
    bias = jnp.transpose(table[:, offset], (1, 2, 0))
    bias = jnp.where(valid[:, :, None], bias, -1e30)

    smem = pl.BlockSpec(memory_space=pltpu.SMEM)
    hbm = pl.BlockSpec(memory_space=pl.ANY)
    vmem = lambda *shape: [pltpu.VMEM((*shape, DH), jnp.bfloat16)] * groups
    unit = math.gcd(tokens, TILE)
    split = (tokens // unit, unit, queries.shape[1])
    dma = pltpu.SemaphoreType.DMA
    return pl.pallas_call(
        functools.partial(attention_kernel, n, blk_count, groups, tokens, slots),
        out_shape=jax.ShapeDtypeStruct(queries.shape, jnp.bfloat16),
        in_specs=[smem, smem, hbm, hbm, hbm],
        out_specs=hbm,
        scratch_shapes=[
            *vmem(3 * frame_tokens // unit, unit),
            *vmem(3 * frame_tokens // unit, unit),
            *vmem(frame_tokens),
            *vmem(frame_tokens),
            pltpu.VMEM((slots // 2, TILE, 2 * TILE), jnp.float32),
            pltpu.VMEM((TILE, 2 * DH), jnp.float32),
            dma((3, groups)),
            dma((3, groups, n)),
            dma((3, groups, n)),
            dma((2, 2, groups, n)),
            dma((2, 2, groups, n)),
            dma((groups, n)),
            dma((groups, n)),
        ],
        compiler_params=pltpu.CompilerParams(
            collective_id=0, has_side_effects=True, vmem_limit_bytes=56 * 1024 * 1024
        ),
        name="attend",
    )(local, bias, queries, keys.reshape(split), values.reshape(split))


def solution(mesh):
    return jax.shard_map(
        on_device,
        mesh=mesh,
        in_specs=(
            P(("dp", "blk", "ulysses"), None),
            P(("dp", "blk", "ulysses"), None),
            P(("dp", "blk", "ulysses"), None),
            P(),
            P(),
            P(),
        ),
        out_specs=P(("dp", "blk", "ulysses"), None),
        check_vma=False,
    )
```
